256 devices in a mesh: dom: 32 (over y, z_lo, core), section: 8 (over x, z_hi).
Axes of the slice: x: 4, y: 4, z: 8 (z_hi: 2, z_lo: 4; z = z_hi * 4 + z_lo), core: 2. Of those that a mesh axis runs over, the one named last changes fastest.
Arguments:
- feats: bfloat16 [131072, 1024], P('dom', 'section'), may hold values from -6 to 6
- tile_vals: bfloat16 [8192, 128, 128], P('dom'), may hold values from -0.1875 to 0.1875
- src_slot: int32 [8192], P('dom'), may hold values from 0 to 95, as said below
- dst_tile: int32 [8192], P('dom'), may hold values from 0 to 31
- tile_count: int32 [32], P('dom'), may hold values from 128 to 256, as said below
- send_tile: int32 [32, 96], P('dom'), may hold values from 0 to 31
- w_fwd: bfloat16 [1024, 1024], replicated, may hold values from -0.1875 to 0.1875
- b_fwd: float32 [1024], replicated, may hold values from -3 to 3
- w_inv1: bfloat16 [1024, 1024], replicated, may hold values from -0.1875 to 0.1875
- b_inv1: float32 [1024], replicated, may hold values from -3 to 3
- w_inv2: bfloat16 [1024, 1024], replicated, may hold values from -0.1875 to 0.1875
- b_inv2: float32 [1024], replicated, may hold values from -3 to 3
- target: bfloat16 [131072, 1024], P(('dom', 'section')), may hold values from -2.5 to 2.5
Outputs:
- hidden: bfloat16 [131072, 1024], P(('dom', 'section'))
- target_prev: bfloat16 [131072, 1024], P(('dom', 'section'))
The draws below stay inside these ranges and needn't reach their ends.
Inputs may be any that keep to these rules, and one draw needn't show every extreme that they name: `src_slot`: slots are numbered by sending partition, 3 each; in each partition's list the entry i names slot number pi(i mod 96) for a permutation pi of the partition. `tile_count`: some partition's list is full.
All inputs are finite; a program needn't handle non-finite values.
Results may differ from the reference program's by a relative error of at most 0.0042.
Values may be sent and summed in bfloat16 or wider, within the bound.
No kernel may reach another device: no remote copies, remote signals or barrier semaphores. Data moves between devices by JAX's collectives and lax.ppermute only.
A program may use at most 192 MiB of HBM per device.

```python
import jax
import jax.numpy as jnp
from jax import lax

D = 1024
TILE = 128
ROWTILES = 32
SLOT = 3
NODES = 131072
LIST = 256
RECV = 96
N_DOM = 32


def draw_src_slot(key, part):
    keys = jax.random.split(key, N_DOM)

    def one_list(single_key):
        order = jax.random.permutation(single_key, RECV)
        return order[jnp.arange(LIST) % RECV]
    return jax.vmap(one_list)(keys).reshape(-1).astype(jnp.int32)


def draw_tile_count(key, part):
    first_key, second_key = jax.random.split(key)
    counts = jax.random.randint(first_key, (N_DOM,), LIST // 2, LIST + 1)
    full_index = jax.random.randint(second_key, (), 0, N_DOM)
    return jnp.where(jnp.arange(N_DOM) == full_index, LIST, counts).astype(jnp.int32)


def place_ends(entries, stream_key, low, high):
    dims = entries.shape
    place = [jax.random.randint(jax.random.fold_in(stream_key, axis), (), 0, dims[axis]) for axis in range(len(dims))]
    entries = entries.at[tuple(place)].set(low)
    longest = dims.index(max(dims))
    place[longest] = (place[longest] + 1) % dims[longest]
    return entries.at[tuple(place)].set(high)


def levels(key, extent, shards, low, high):
    def one(axis_at, parts):
        draws = jax.random.uniform(jax.random.fold_in(jax.random.fold_in(key, 6), axis_at), (parts,), jnp.float32, low / len(shards), high / len(shards))
        return jnp.repeat(jnp.exp(draws), extent[axis_at] // parts).reshape((-1,) + (1,) * (len(extent) - axis_at - 1))

    loudness = one(*shards[0])
    for cut in shards[1:]:
        loudness = loudness * one(*cut)
    return loudness


def bell_draw(own_key, dims, deviation, limit, shards=(), kind=jnp.bfloat16):
    drawn = jax.random.normal(own_key, dims, jnp.float32) * deviation
    if len(shards) > 0:
        drawn = levels(own_key, dims, shards, -0.22, 0.18) * drawn
    return jnp.clip(drawn, min=-limit, max=limit).astype(kind)


def setup_inputs(seed: int = 0) -> dict:
    key_of = jax.random.split(jax.random.key(seed), 14)
    return {
        "feats": bell_draw(key_of[0], (NODES, D), 1.0, 6.0, ((0, 32), (1, 8))),
        "tile_vals": bell_draw(key_of[1], (N_DOM * LIST, TILE, TILE), (8 * TILE) ** -0.5, 0.1875, ((0, 32),)),
        "src_slot": draw_src_slot(jax.random.fold_in(key_of[13], 71), 0),
        "dst_tile": place_ends(jax.random.randint(key_of[3], (N_DOM * LIST,), 0, ROWTILES), jax.random.fold_in(key_of[3], 1), 0, ROWTILES - 1).astype(jnp.int32),
        "tile_count": draw_tile_count(jax.random.fold_in(key_of[13], 71), 0),
        "send_tile": place_ends(jax.random.randint(key_of[5], (N_DOM, RECV), 0, ROWTILES), jax.random.fold_in(key_of[5], 1), 0, ROWTILES - 1).astype(jnp.int32),
        "w_fwd": bell_draw(key_of[6], (D, D), D ** -0.5, 0.1875),
        "b_fwd": bell_draw(key_of[7], (D,), 0.5, 3.0, (), jnp.float32),
        "w_inv1": bell_draw(key_of[8], (D, D), D ** -0.5, 0.1875),
        "b_inv1": bell_draw(key_of[9], (D,), 0.5, 3.0, (), jnp.float32),
        "w_inv2": bell_draw(key_of[10], (D, D), D ** -0.5, 0.1875),
        "b_inv2": bell_draw(key_of[11], (D,), 0.5, 3.0, (), jnp.float32),
        "target": bell_draw(key_of[12], (NODES, D), 0.6, 2.5, ((0, 256),)),
    }


def reference(feats, tile_vals, src_slot, dst_tile, tile_count, send_tile, w_fwd, b_fwd, w_inv1, b_inv1, w_inv2, b_inv2, target):
    flat_blocks = feats.reshape(N_DOM * ROWTILES, TILE, D)

    def one_part(part_index):
        my_slots = lax.dynamic_slice_in_dim(send_tile, part_index * SLOT, SLOT, 1).astype(jnp.int32)
        owners = jnp.arange(N_DOM, dtype=jnp.int32)[:, None] * ROWTILES + my_slots
        received = flat_blocks[owners.reshape(-1)]
        values_part = lax.dynamic_slice_in_dim(tile_vals, part_index * LIST, LIST, 0)
        slot_part = lax.dynamic_slice_in_dim(src_slot, part_index * LIST, LIST, 0)
        dest_part = lax.dynamic_slice_in_dim(dst_tile, part_index * LIST, LIST, 0)
        live_count = lax.dynamic_slice_in_dim(tile_count, part_index, 1, 0)[0]
        products = jnp.einsum("lab,lbc->lac", values_part.astype(jnp.float32), received[slot_part].astype(jnp.float32), precision=lax.Precision.HIGHEST)
        active = jnp.arange(LIST, dtype=jnp.int32) < live_count
        onehot = ((dest_part[None, :] == jnp.arange(ROWTILES, dtype=jnp.int32)[:, None]) & active[None, :]).astype(jnp.float32)
        summed = jnp.dot(onehot, products.reshape(LIST, TILE * D), precision=lax.Precision.HIGHEST)
        return summed.reshape(ROWTILES * TILE, D).astype(jnp.bfloat16)

    agg = lax.map(one_part, jnp.arange(N_DOM, dtype=jnp.int32)).reshape(N_DOM * ROWTILES * TILE, D)
    hidden = jnp.tanh(jnp.dot(agg, w_fwd, preferred_element_type=jnp.float32) + b_fwd).astype(jnp.bfloat16)

    def inverse(values):
        inner = jnp.tanh(jnp.dot(values, w_inv1, preferred_element_type=jnp.float32) + b_inv1).astype(jnp.bfloat16)
        return jnp.tanh(jnp.dot(inner, w_inv2, preferred_element_type=jnp.float32) + b_inv2)

    shifted = feats.astype(jnp.float32) + inverse(target) - inverse(hidden)
    return hidden, shifted.astype(jnp.bfloat16)
```

```python
import jax
import jax.numpy as jnp
from jax import lax
from jax.experimental import pallas as pl
from jax.experimental.pallas import tpu as pltpu
from jax.sharding import PartitionSpec as P

CHUNK = 16
UNROLL = 4


def pack_tiles(feats, send_ids):
    row_tiles, side, cols = feats.shape
    slots = send_ids.shape[0]

    def body(ids, src, out, sem):
        def issue(i, _):
            pltpu.make_async_copy(src.at[ids[i]], out.at[i], sem).start()
            return 0

        lax.fori_loop(0, slots, issue, 0, unroll=8)
        pltpu.make_async_copy(out, out, sem).wait()

    return pl.pallas_call(
        body,
        grid_spec=pltpu.PrefetchScalarGridSpec(
            num_scalar_prefetch=1,
            grid=(1,),
            in_specs=[pl.BlockSpec((row_tiles, side, cols), lambda i, ids: (0, 0, 0))],
            out_specs=pl.BlockSpec(memory_space=pl.ANY),
            scratch_shapes=[pltpu.SemaphoreType.DMA],
        ),
        out_shape=jax.ShapeDtypeStruct((slots, side, cols), feats.dtype),
        name="pack_tiles",
    )(send_ids, feats)


def aggregate(received, tile_vals, src_slot, dst_tile, tile_count, row_tiles):
    slots, side, cols = received.shape
    entries = tile_vals.shape[0]
    levels = pl.cdiv(entries, slots)
    tail = entries - (levels - 1) * slots
    chunks = slots // CHUNK

    def copies(vals, store, sems, chunk):
        base = chunk * CHUNK
        out = []
        for level in range(levels):
            if level == levels - 1 and base >= tail:
                continue
            out.append(
                pltpu.make_async_copy(
                    vals.at[pl.ds(level * slots + base, CHUNK)],
                    store.at[pl.ds(base, CHUNK), level],
                    sems.at[chunk, level],
                )
            )
        return out

    def body(slot_ref, dst_ref, count_ref, recv, vals, out, store, acc, sems):
        for chunk in range(chunks):
            for copy in copies(vals, store, sems, chunk):
                copy.start()
        acc[...] = jnp.zeros_like(acc)
        count = count_ref[0]
        for chunk in range(chunks):
            waits = copies(vals, store, sems, chunk)
            for copy in waits:
                copy.wait()
            live_levels = len(waits)

            def step(turn, _):
                for k in range(UNROLL):
                    j = chunk * CHUNK + turn * UNROLL + k
                    source = recv[slot_ref[j]]
                    left = store[j, :live_levels].reshape(live_levels * side, side)
                    product = jnp.dot(left, source, preferred_element_type=jnp.float32)
                    for level in range(live_levels):
                        i = j + level * slots
                        place = jnp.where(i < count, dst_ref[i], row_tiles)
                        acc[place] += product[level * side : (level + 1) * side]
                return 0

            lax.fori_loop(0, CHUNK // UNROLL, step, 0)
        for tile in range(row_tiles):
            out[tile] = acc[tile].astype(out.dtype)

    return pl.pallas_call(
        body,
        grid_spec=pltpu.PrefetchScalarGridSpec(
            num_scalar_prefetch=3,
            grid=(1,),
            in_specs=[
                pl.BlockSpec((slots, side, cols), lambda i, *_: (0, 0, 0)),
                pl.BlockSpec(memory_space=pl.ANY),
            ],
            out_specs=pl.BlockSpec((row_tiles, side, cols), lambda i, *_: (0, 0, 0)),
            scratch_shapes=[
                pltpu.VMEM((slots, levels, side, side), tile_vals.dtype),
                pltpu.VMEM((row_tiles + 1, side, cols), jnp.float32),
                pltpu.SemaphoreType.DMA((chunks, levels)),
            ],
        ),
        out_shape=jax.ShapeDtypeStruct((row_tiles, side, cols), received.dtype),
        compiler_params=pltpu.CompilerParams(vmem_limit_bytes=32 << 20),
        cost_estimate=pl.CostEstimate(
            flops=2 * entries * side * side * cols,
            bytes_accessed=entries * side * side * 2 + (slots + row_tiles) * side * cols * 2,
            transcendentals=0,
        ),
        name="aggregate",
    )(src_slot, dst_tile, tile_count, received, tile_vals)


def finish(agg, inputs, g_target, w_fwd, b_fwd, w_inv1, b_inv1, w_inv2, b_inv2):
    groups, rows, cols = agg.shape
    width = groups * cols
    block = 256

    def body(agg_ref, in_ref, gt_ref, wf, bf, w1, b1, w2, b2, hid_ref, out_ref):
        rows_in = jnp.concatenate([agg_ref[g] for g in range(groups)], axis=1)
        hidden = jnp.tanh(jnp.dot(rows_in, wf[...], preferred_element_type=jnp.float32) + bf[...])
        hidden = hidden.astype(hid_ref.dtype)
        hid_ref[...] = hidden
        inner = jnp.tanh(jnp.dot(hidden, w1[...], preferred_element_type=jnp.float32) + b1[...])
        inner = inner.astype(hid_ref.dtype)
        back = jnp.tanh(jnp.dot(inner, w2[...], preferred_element_type=jnp.float32) + b2[...])
        feats = jnp.concatenate([in_ref[g] for g in range(groups)], axis=1).astype(jnp.float32)
        out_ref[...] = (feats + gt_ref[...] - back).astype(out_ref.dtype)

    split = pl.BlockSpec((groups, block, cols), lambda i: (0, i, 0))
    whole = pl.BlockSpec((block, width), lambda i: (i, 0))
    weight = pl.BlockSpec((width, width), lambda i: (0, 0))
    bias = pl.BlockSpec((1, width), lambda i: (0, 0))
    return pl.pallas_call(
        body,
        grid=(rows // block,),
        in_specs=[split, split, whole, weight, bias, weight, bias, weight, bias],
        out_specs=[whole, whole],
        out_shape=[jax.ShapeDtypeStruct((rows, width), agg.dtype)] * 2,
        compiler_params=pltpu.CompilerParams(vmem_limit_bytes=40 << 20),
        cost_estimate=pl.CostEstimate(
            flops=6 * rows * width * width,
            bytes_accessed=6 * width * width + 12 * rows * width,
            transcendentals=3 * rows * width,
        ),
        name="finish",
    )(agg, inputs, g_target, w_fwd, b_fwd[None], w_inv1, b_inv1[None], w_inv2, b_inv2[None])


def per_device(
    feats,
    tile_vals,
    src_slot,
    dst_tile,
    tile_count,
    send_tile,
    w_fwd,
    b_fwd,
    w_inv1,
    b_inv1,
    w_inv2,
    b_inv2,
    target,
):
    node_rows, feat_cols = feats.shape
    side = tile_vals.shape[1]
    row_tiles = node_rows // side
    rows = target.shape[0]
    groups = node_rows // rows
    outgoing = pack_tiles(feats.reshape(row_tiles, side, feat_cols), send_tile[0])
    received = lax.all_to_all(outgoing, "dom", split_axis=0, concat_axis=0, tiled=True)
    inner = jnp.tanh(jnp.dot(target, w_inv1, preferred_element_type=jnp.float32) + b_inv1).astype(
        jnp.bfloat16
    )
    g_target = jnp.tanh(jnp.dot(inner, w_inv2, preferred_element_type=jnp.float32) + b_inv2)
    received, g_target = lax.optimization_barrier((received, g_target))
    agg = aggregate(received, tile_vals, src_slot, dst_tile, tile_count, row_tiles)
    agg_rows = lax.all_to_all(
        agg.reshape(groups, rows, feat_cols), "section", split_axis=0, concat_axis=0, tiled=True
    )
    input_rows = lax.all_to_all(
        feats.reshape(groups, rows, feat_cols), "section", split_axis=0, concat_axis=0, tiled=True
    )
    hidden, shifted = finish(
        agg_rows, input_rows, g_target, w_fwd, b_fwd, w_inv1, b_inv1, w_inv2, b_inv2
    )
    return (hidden, shifted)


def solution(mesh):
    placed = (
        P("dom", "section"),
        P("dom", None, None),
        P("dom"),
        P("dom"),
        P("dom"),
        P("dom", None),
        P(),
        P(),
        P(),
        P(),
        P(),
        P(),
        P(("dom", "section"), None),
    )
    return jax.shard_map(
        per_device,
        mesh=mesh,
        in_specs=placed,
        out_specs=(P(("dom", "section"), None), P(("dom", "section"), None)),
        check_vma=False,
    )
```

```python
import jax
import jax.numpy as jnp
from jax import lax
from jax.experimental import pallas as pl
from jax.experimental.pallas import tpu as pltpu
from jax.sharding import PartitionSpec as P

CHUNK = 16
UNROLL = 16


def pack_tiles(feats, send_ids):
    row_tiles, side, cols = feats.shape
    slots = send_ids.shape[0]

    def body(ids, src, out, sem):
        def issue(i, _):
            pltpu.make_async_copy(src.at[ids[i]], out.at[i], sem).start()
            return 0

        lax.fori_loop(0, slots, issue, 0, unroll=8)
        pltpu.make_async_copy(out, out, sem).wait()

    return pl.pallas_call(
        body,
        grid_spec=pltpu.PrefetchScalarGridSpec(
            num_scalar_prefetch=1,
            grid=(1,),
            in_specs=[pl.BlockSpec((row_tiles, side, cols), lambda i, ids: (0, 0, 0))],
            out_specs=pl.BlockSpec(memory_space=pl.ANY),
            scratch_shapes=[pltpu.SemaphoreType.DMA],
        ),
        out_shape=jax.ShapeDtypeStruct((slots, side, cols), feats.dtype),
        compiler_params=pltpu.CompilerParams(vmem_limit_bytes=56 << 20),
        name="pack_tiles",
    )(send_ids, feats)


def own_pieces(feats, me, groups):
    row_tiles, side, cols = feats.shape
    per = row_tiles // groups
    half = groups // 2

    def body(me_ref, src, far, *near):
        for m in range(half):
            near[m][...] = src[pl.ds((me_ref[0] ^ (2 * m)) * per, per)]
            far[m] = src[pl.ds((me_ref[0] ^ (2 * m + 1)) * per, per)]

    piece = (per, side, cols)
    shapes = [(half,) + piece] + [piece] * half
    made = pl.pallas_call(
        body,
        grid_spec=pltpu.PrefetchScalarGridSpec(
            num_scalar_prefetch=1,
            grid=(1,),
            in_specs=[pl.BlockSpec((row_tiles, side, cols), lambda i, *_: (0, 0, 0))],
            out_specs=[pl.BlockSpec(n, lambda i, *_, z=len(n): (0,) * z) for n in shapes],
        ),
        out_shape=[jax.ShapeDtypeStruct(n, feats.dtype) for n in shapes],
        name="own_pieces",
    )(me, feats)
    return made[0], made[1:]


def aggregate(received, tile_vals, after, src_slot, dst_tile, tile_count, me, row_tiles, groups):
    slots, side, cols = received.shape
    entries = tile_vals.shape[0]
    levels = pl.cdiv(entries, slots)
    tail = entries - (levels - 1) * slots
    chunks = slots // CHUNK
    per = row_tiles // groups

    def copies(vals, store, sems, chunk):
        base = chunk * CHUNK
        out = []
        for level in range(levels):
            if level == levels - 1 and base >= tail:
                continue
            out.append(
                pltpu.make_async_copy(
                    vals.at[pl.ds(level * slots + base, CHUNK)],
                    store.at[pl.ds(base, CHUNK), level],
                    sems.at[chunk, level],
                )
            )
        return out

    def body(slot_ref, dst_ref, count_ref, me_ref, recv_hbm, vals, _, *rest):
        pieces, (recv, store, acc, sems, recv_sem) = rest[:groups], rest[groups:]
        arrive = pltpu.make_async_copy(recv_hbm, recv, recv_sem)
        arrive.start()
        for chunk in range(chunks):
            for copy in copies(vals, store, sems, chunk):
                copy.start()
        acc[...] = jnp.zeros_like(acc)
        count = count_ref[0]
        arrive.wait()
        for chunk in range(chunks):
            waits = copies(vals, store, sems, chunk)
            for copy in waits:
                copy.wait()
            live_levels = len(waits)

            def step(turn, _):
                for k in range(UNROLL):
                    j = chunk * CHUNK + turn * UNROLL + k
                    source = recv[slot_ref[j]]
                    left = store[j, :live_levels].reshape(live_levels * side, side)
                    product = jnp.dot(left, source, preferred_element_type=jnp.float32)
                    for level in range(live_levels):
                        i = j + level * slots
                        place = jnp.where(i < count, dst_ref[i], row_tiles)
                        acc[place] += product[level * side : (level + 1) * side]
                return 0

            lax.fori_loop(0, CHUNK // UNROLL, step, 0)
        for k in range(groups):
            there = (me_ref[0] ^ k) * per
            for tile in range(per):
                pieces[k][tile] = acc[there + tile].astype(pieces[k].dtype)

    return pl.pallas_call(
        body,
        grid_spec=pltpu.PrefetchScalarGridSpec(
            num_scalar_prefetch=4,
            grid=(1,),
            in_specs=[
                pl.BlockSpec(memory_space=pl.ANY),
                pl.BlockSpec(memory_space=pl.ANY),
                pl.BlockSpec(memory_space=pltpu.VMEM),
            ],
            out_specs=[pl.BlockSpec((per, side, cols), lambda i, *_: (0, 0, 0))] * groups,
            scratch_shapes=[
                pltpu.VMEM((slots, side, cols), received.dtype),
                pltpu.VMEM((slots, levels, side, side), tile_vals.dtype),
                pltpu.VMEM((row_tiles + 1, side, cols), jnp.float32),
                pltpu.SemaphoreType.DMA((chunks, levels)),
                pltpu.SemaphoreType.DMA,
            ],
        ),
        out_shape=[jax.ShapeDtypeStruct((per, side, cols), received.dtype)] * groups,
        compiler_params=pltpu.CompilerParams(vmem_limit_bytes=52 << 20),
        cost_estimate=pl.CostEstimate(
            flops=8 * entries * side * side * cols,
            bytes_accessed=entries * side * side * 2 + (slots + row_tiles) * side * cols * 2,
            transcendentals=0,
        ),
        name="aggregate",
    )(src_slot, dst_tile, tile_count, me, received, tile_vals, after)


def finish(agg, inputs, me, g_target, w_fwd, b_fwd, w_inv1, b_inv1, w_inv2, b_inv2):
    groups = len(agg)
    rows, cols = agg[0].shape
    width = groups * cols
    block = 256

    def body(me_ref, *refs):
        agg_refs, in_refs = refs[:groups], refs[groups : 2 * groups]
        gt_ref, wf, bf, w1, b1, w2, b2, hid_ref, out_ref, rows_agg, rows_in = refs[2 * groups :]
        for k in range(groups):
            where = pl.ds(pl.multiple_of((me_ref[0] ^ k) * cols, cols), cols)
            rows_agg[:, where] = agg_refs[k][...]
            rows_in[:, where] = in_refs[k][...]
        hidden = jnp.tanh(
            jnp.dot(rows_agg[...], wf[...], preferred_element_type=jnp.float32) + bf[...]
        )
        hidden = hidden.astype(hid_ref.dtype)
        hid_ref[...] = hidden
        inner = jnp.tanh(jnp.dot(hidden, w1[...], preferred_element_type=jnp.float32) + b1[...])
        inner = inner.astype(hid_ref.dtype)
        back = jnp.tanh(jnp.dot(inner, w2[...], preferred_element_type=jnp.float32) + b2[...])
        out_ref[...] = (rows_in[...].astype(jnp.float32) + gt_ref[...] - back).astype(out_ref.dtype)

    piece = pl.BlockSpec((block, cols), lambda i, *_: (i, 0))
    whole = pl.BlockSpec((block, width), lambda i, *_: (i, 0))
    weight = pl.BlockSpec((width, width), lambda i, *_: (0, 0))
    bias = pl.BlockSpec((1, width), lambda i, *_: (0, 0))
    return pl.pallas_call(
        body,
        grid_spec=pltpu.PrefetchScalarGridSpec(
            num_scalar_prefetch=1,
            grid=(rows // block,),
            in_specs=[piece] * (2 * groups) + [whole, weight, bias, weight, bias, weight, bias],
            out_specs=[whole, whole],
            scratch_shapes=[pltpu.VMEM((block, width), agg[0].dtype)] * 2,
        ),
        out_shape=[jax.ShapeDtypeStruct((rows, width), agg[0].dtype)] * 2,
        compiler_params=pltpu.CompilerParams(vmem_limit_bytes=40 << 20),
        cost_estimate=pl.CostEstimate(
            flops=6 * rows * width * width,
            bytes_accessed=6 * width * width + 12 * rows * width,
            transcendentals=3 * rows * width,
        ),
        name="finish",
    )(me, *agg, *inputs, g_target, w_fwd, b_fwd[None], w_inv1, b_inv1[None], w_inv2, b_inv2[None])


def exchange(pieces, groups):
    order = [k for k in range(groups) if k % 2] + [k for k in range(2, groups, 2)]
    back = [pieces[0]] + [None] * (groups - 1)
    for k in order:
        back[k] = lax.ppermute(pieces[k], "section", [(s, s ^ k) for s in range(groups)])
    return back


def swap(piece, k, groups):
    return lax.ppermute(piece, "section", [(s, s ^ k) for s in range(groups)])


def per_device(
    feats,
    tile_vals,
    src_slot,
    dst_tile,
    tile_count,
    send_tile,
    w_fwd,
    b_fwd,
    w_inv1,
    b_inv1,
    w_inv2,
    b_inv2,
    target,
):
    node_rows, feat_cols = feats.shape
    side = tile_vals.shape[1]
    row_tiles = node_rows // side
    rows = target.shape[0]
    groups = node_rows // rows
    me = lax.axis_index("section").astype(jnp.int32)[None]
    tiles = feats.reshape(row_tiles, side, feat_cols)
    outgoing = pack_tiles(tiles, send_tile[0])
    received = lax.all_to_all(outgoing, "dom", split_axis=0, concat_axis=0, tiled=True)
    inner = jnp.tanh(jnp.dot(target, w_inv1, preferred_element_type=jnp.float32) + b_inv1).astype(
        jnp.bfloat16
    )
    g_target = jnp.tanh(jnp.dot(inner, w_inv2, preferred_element_type=jnp.float32) + b_inv2)
    far, near = own_pieces(tiles, me, groups)
    near = [near[0]] + [swap(near[m], 2 * m, groups) for m in range(1, groups // 2)]
    far, after = lax.optimization_barrier((far, received[0, :8] + g_target[:8, :feat_cols]))
    far = swap(far, 1, groups)
    agg = aggregate(
        received, tile_vals, after, src_slot, dst_tile, tile_count, me, row_tiles, groups
    )
    input_rows = [near[0], far[0]]
    for m in range(1, groups // 2):
        input_rows += [near[m], swap(far[m], 2 * m, groups)]
    agg_rows = exchange(agg, groups)
    flat = lambda pieces: [p.reshape(rows, feat_cols) for p in pieces]
    hidden, shifted = finish(
        flat(agg_rows), flat(input_rows), me, g_target, w_fwd, b_fwd, w_inv1, b_inv1, w_inv2, b_inv2
    )
    return (hidden, shifted)


def solution(mesh):
    placed = (
        P("dom", "section"),
        P("dom", None, None),
        P("dom"),
        P("dom"),
        P("dom"),
        P("dom", None),
        P(),
        P(),
        P(),
        P(),
        P(),
        P(),
        P(("dom", "section"), None),
    )
    return jax.shard_map(
        per_device,
        mesh=mesh,
        in_specs=placed,
        out_specs=(P(("dom", "section"), None), P(("dom", "section"), None)),
        check_vma=False,
    )
```

```python
import jax
import jax.numpy as jnp
from jax import lax
from jax.experimental import pallas as pl
from jax.experimental.pallas import tpu as pltpu
from jax.sharding import PartitionSpec as P

CHUNK = 16
UNROLL = 16


def pack_tiles(feats, send_ids):
    row_tiles, side, cols = feats.shape
    slots = send_ids.shape[0]

    def body(ids, src, out, sem):
        def issue(i, _):
            pltpu.make_async_copy(src.at[ids[i]], out.at[i], sem).start()
            return 0

        lax.fori_loop(0, slots, issue, 0, unroll=8)
        pltpu.make_async_copy(out, out, sem).wait()

    return pl.pallas_call(
        body,
        grid_spec=pltpu.PrefetchScalarGridSpec(
            num_scalar_prefetch=1,
            grid=(1,),
            in_specs=[pl.BlockSpec(memory_space=pl.ANY)],
            out_specs=pl.BlockSpec(memory_space=pl.ANY),
            scratch_shapes=[pltpu.SemaphoreType.DMA],
        ),
        out_shape=jax.ShapeDtypeStruct((slots, side, cols), feats.dtype),
        compiler_params=pltpu.CompilerParams(vmem_limit_bytes=56 << 20),
        name="pack_tiles",
    )(send_ids, feats)


def own_pieces(feats, me, groups):
    row_tiles, side, cols = feats.shape
    per = row_tiles // groups
    half = groups // 2

    def body(me_ref, src, far, *near):
        for m in range(half):
            near[m][...] = src[pl.ds((me_ref[0] ^ (2 * m)) * per, per)]
            far[m] = src[pl.ds((me_ref[0] ^ (2 * m + 1)) * per, per)]

    piece = (per, side, cols)
    shapes = [(half,) + piece] + [piece] * half
    made = pl.pallas_call(
        body,
        grid_spec=pltpu.PrefetchScalarGridSpec(
            num_scalar_prefetch=1,
            grid=(1,),
            in_specs=[pl.BlockSpec((row_tiles, side, cols), lambda i, *_: (0, 0, 0))],
            out_specs=[pl.BlockSpec(n, lambda i, *_, z=len(n): (0,) * z) for n in shapes],
        ),
        out_shape=[jax.ShapeDtypeStruct(n, feats.dtype) for n in shapes],
        name="own_pieces",
    )(me, feats)
    return made[0], made[1:]


def aggregate(received, tile_vals, after, src_slot, dst_tile, tile_count, me, row_tiles, groups):
    slots, side, cols = received.shape
    entries = tile_vals.shape[0]
    levels = pl.cdiv(entries, slots)
    tail = entries - (levels - 1) * slots
    chunks = slots // CHUNK
    per = row_tiles // groups

    def copies(vals, store, sems, chunk):
        base = chunk * CHUNK
        out = []
        for level in range(levels):
            if level == levels - 1 and base >= tail:
                continue
            out.append(
                pltpu.make_async_copy(
                    vals.at[pl.ds(level * slots + base, CHUNK)],
                    store.at[pl.ds(base, CHUNK), level],
                    sems.at[chunk, level],
                )
            )
        return out

    def body(slot_ref, dst_ref, count_ref, me_ref, recv_hbm, vals, _, *rest):
        pieces, (recv, store, acc, sems, recv_sem) = rest[:groups], rest[groups:]
        arrive = pltpu.make_async_copy(recv_hbm, recv, recv_sem)
        arrive.start()
        for chunk in range(chunks):
            for copy in copies(vals, store, sems, chunk):
                copy.start()
        acc[...] = jnp.zeros_like(acc)
        count = count_ref[0]
        arrive.wait()
        for chunk in range(chunks):
            waits = copies(vals, store, sems, chunk)
            for copy in waits:
                copy.wait()
            live_levels = len(waits)

            def step(turn, _):
                for k in range(UNROLL):
                    j = chunk * CHUNK + turn * UNROLL + k
                    source = recv[slot_ref[j]]
                    left = store[j, :live_levels].reshape(live_levels * side, side)
                    product = jnp.dot(left, source, preferred_element_type=jnp.float32)
                    for level in range(live_levels):
                        i = j + level * slots
                        place = jnp.where(i < count, dst_ref[i], row_tiles)
                        acc[place] += product[level * side : (level + 1) * side]
                return 0

            lax.fori_loop(0, CHUNK // UNROLL, step, 0)
        for k in range(groups):
            there = (me_ref[0] ^ k) * per
            for tile in range(per):
                pieces[k][tile] = acc[there + tile].astype(pieces[k].dtype)

    return pl.pallas_call(
        body,
        grid_spec=pltpu.PrefetchScalarGridSpec(
            num_scalar_prefetch=4,
            grid=(1,),
            in_specs=[
                pl.BlockSpec(memory_space=pl.ANY),
                pl.BlockSpec(memory_space=pl.ANY),
                pl.BlockSpec(memory_space=pltpu.VMEM),
            ],
            out_specs=[pl.BlockSpec((per, side, cols), lambda i, *_: (0, 0, 0))] * groups,
            scratch_shapes=[
                pltpu.VMEM((slots, side, cols), received.dtype),
                pltpu.VMEM((slots, levels, side, side), tile_vals.dtype),
                pltpu.VMEM((row_tiles + 1, side, cols), jnp.float32),
                pltpu.SemaphoreType.DMA((chunks, levels)),
                pltpu.SemaphoreType.DMA,
            ],
        ),
        out_shape=[jax.ShapeDtypeStruct((per, side, cols), received.dtype)] * groups,
        compiler_params=pltpu.CompilerParams(vmem_limit_bytes=52 << 20),
        cost_estimate=pl.CostEstimate(
            flops=8 * entries * side * side * cols,
            bytes_accessed=entries * side * side * 2 + (slots + row_tiles) * side * cols * 2,
            transcendentals=0,
        ),
        name="aggregate",
    )(src_slot, dst_tile, tile_count, me, received, tile_vals, after)


def finish(agg, inputs, me, g_target, w_fwd, b_fwd, w_inv1, b_inv1, w_inv2, b_inv2):
    groups = len(agg)
    rows, cols = agg[0].shape
    width = groups * cols
    block = 256

    def body(me_ref, *refs):
        agg_refs, in_refs = refs[:groups], refs[groups : 2 * groups]
        gt_ref, wf, bf, w1, b1, w2, b2, hid_ref, out_ref, rows_agg, rows_in = refs[2 * groups :]
        for k in range(groups):
            where = pl.ds(pl.multiple_of((me_ref[0] ^ k) * cols, cols), cols)
            rows_agg[:, where] = agg_refs[k][...]
            rows_in[:, where] = in_refs[k][...]
        hidden = jnp.tanh(
            jnp.dot(rows_agg[...], wf[...], preferred_element_type=jnp.float32) + bf[...]
        )
        hidden = hidden.astype(hid_ref.dtype)
        hid_ref[...] = hidden
        inner = jnp.tanh(jnp.dot(hidden, w1[...], preferred_element_type=jnp.float32) + b1[...])
        inner = inner.astype(hid_ref.dtype)
        back = jnp.tanh(jnp.dot(inner, w2[...], preferred_element_type=jnp.float32) + b2[...])
        out_ref[...] = (rows_in[...].astype(jnp.float32) + gt_ref[...] - back).astype(out_ref.dtype)

    piece = pl.BlockSpec((block, cols), lambda i, *_: (i, 0))
    whole = pl.BlockSpec((block, width), lambda i, *_: (i, 0))
    weight = pl.BlockSpec((width, width), lambda i, *_: (0, 0))
    bias = pl.BlockSpec((1, width), lambda i, *_: (0, 0))
    return pl.pallas_call(
        body,
        grid_spec=pltpu.PrefetchScalarGridSpec(
            num_scalar_prefetch=1,
            grid=(rows // block,),
            in_specs=[piece] * (2 * groups) + [whole, weight, bias, weight, bias, weight, bias],
            out_specs=[whole, whole],
            scratch_shapes=[pltpu.VMEM((block, width), agg[0].dtype)] * 2,
        ),
        out_shape=[jax.ShapeDtypeStruct((rows, width), agg[0].dtype)] * 2,
        compiler_params=pltpu.CompilerParams(vmem_limit_bytes=40 << 20),
        cost_estimate=pl.CostEstimate(
            flops=6 * rows * width * width,
            bytes_accessed=6 * width * width + 12 * rows * width,
            transcendentals=3 * rows * width,
        ),
        name="finish",
    )(me, *agg, *inputs, g_target, w_fwd, b_fwd[None], w_inv1, b_inv1[None], w_inv2, b_inv2[None])


def exchange(pieces, groups):
    order = [k for k in range(groups) if k % 2] + [k for k in range(2, groups, 2)]
    back = [pieces[0]] + [None] * (groups - 1)
    for k in order:
        back[k] = lax.ppermute(pieces[k], "section", [(s, s ^ k) for s in range(groups)])
    return back


def swap(piece, k, groups):
    return lax.ppermute(piece, "section", [(s, s ^ k) for s in range(groups)])


def per_device(
    feats,
    tile_vals,
    src_slot,
    dst_tile,
    tile_count,
    send_tile,
    w_fwd,
    b_fwd,
    w_inv1,
    b_inv1,
    w_inv2,
    b_inv2,
    target,
):
    node_rows, feat_cols = feats.shape
    side = tile_vals.shape[1]
    row_tiles = node_rows // side
    rows = target.shape[0]
    groups = node_rows // rows
    me = lax.axis_index("section").astype(jnp.int32)[None]
    tiles = feats.reshape(row_tiles, side, feat_cols)
    outgoing = pack_tiles(tiles, send_tile[0])
    received = lax.all_to_all(outgoing, "dom", split_axis=0, concat_axis=0, tiled=True)
    inner = jnp.tanh(jnp.dot(target, w_inv1, preferred_element_type=jnp.float32) + b_inv1).astype(
        jnp.bfloat16
    )
    g_target = jnp.tanh(jnp.dot(inner, w_inv2, preferred_element_type=jnp.float32) + b_inv2)
    far, near = own_pieces(tiles, me, groups)
    near = [near[0]] + [swap(near[m], 2 * m, groups) for m in range(1, groups // 2)]
    far, after = lax.optimization_barrier((far, received[0, :8] + g_target[:8, :feat_cols]))
    far = swap(far, 1, groups)
    agg = aggregate(
        received, tile_vals, after, src_slot, dst_tile, tile_count, me, row_tiles, groups
    )
    input_rows = [near[0], far[0]]
    for m in range(1, groups // 2):
        input_rows += [near[m], swap(far[m], 2 * m, groups)]
    agg_rows = exchange(agg, groups)
    flat = lambda pieces: [p.reshape(rows, feat_cols) for p in pieces]
    hidden, shifted = finish(
        flat(agg_rows), flat(input_rows), me, g_target, w_fwd, b_fwd, w_inv1, b_inv1, w_inv2, b_inv2
    )
    return (hidden, shifted)


def solution(mesh):
    placed = (
        P("dom", "section"),
        P("dom", None, None),
        P("dom"),
        P("dom"),
        P("dom"),
        P("dom", None),
        P(),
        P(),
        P(),
        P(),
        P(),
        P(),
        P(("dom", "section"), None),
    )
    return jax.shard_map(
        per_device,
        mesh=mesh,
        in_specs=placed,
        out_specs=(P(("dom", "section"), None), P(("dom", "section"), None)),
        check_vma=False,
    )
```

```python
import jax
import jax.numpy as jnp
from jax import lax
from jax.experimental import pallas as pl
from jax.experimental.pallas import tpu as pltpu
from jax.sharding import PartitionSpec as P

CHUNK = 16
UNROLL = 16


def pack_tiles(feats, send_ids):
    row_tiles, side, cols = feats.shape
    slots = send_ids.shape[0]

    def body(ids, src, out):
        def step(i, _):
            out[i] = src[ids[i]]
            return 0

        lax.fori_loop(0, slots, step, 0, unroll=8)

    return pl.pallas_call(
        body,
        grid_spec=pltpu.PrefetchScalarGridSpec(
            num_scalar_prefetch=1,
            grid=(1,),
            in_specs=[pl.BlockSpec((row_tiles, side, cols), lambda i, ids: (0, 0, 0))],
            out_specs=pl.BlockSpec((slots, side, cols), lambda i, ids: (0, 0, 0)),
        ),
        out_shape=jax.ShapeDtypeStruct((slots, side, cols), feats.dtype),
        compiler_params=pltpu.CompilerParams(vmem_limit_bytes=56 << 20),
        name="pack_tiles",
    )(send_ids, feats)


def own_pieces(feats, me, groups):
    row_tiles, side, cols = feats.shape
    per = row_tiles // groups
    half = groups // 2

    def body(me_ref, src, far, *near):
        for m in range(half):
            near[m][...] = src[pl.ds((me_ref[0] ^ (2 * m)) * per, per)]
            far[m] = src[pl.ds((me_ref[0] ^ (2 * m + 1)) * per, per)]

    piece = (per, side, cols)
    shapes = [(half,) + piece] + [piece] * half
    made = pl.pallas_call(
        body,
        grid_spec=pltpu.PrefetchScalarGridSpec(
            num_scalar_prefetch=1,
            grid=(1,),
            in_specs=[pl.BlockSpec((row_tiles, side, cols), lambda i, *_: (0, 0, 0))],
            out_specs=[pl.BlockSpec(n, lambda i, *_, z=len(n): (0,) * z) for n in shapes],
        ),
        out_shape=[jax.ShapeDtypeStruct(n, feats.dtype) for n in shapes],
        name="own_pieces",
    )(me, feats)
    return made[0], made[1:]


def aggregate(received, tile_vals, after, src_slot, dst_tile, tile_count, me, row_tiles, groups):
    slots, side, cols = received.shape
    entries = tile_vals.shape[0]
    levels = pl.cdiv(entries, slots)
    tail = entries - (levels - 1) * slots
    chunks = slots // CHUNK
    per = row_tiles // groups

    def copies(vals, store, sems, chunk):
        base = chunk * CHUNK
        out = []
        for level in range(levels):
            if level == levels - 1 and base >= tail:
                continue
            out.append(
                pltpu.make_async_copy(
                    vals.at[pl.ds(level * slots + base, CHUNK)],
                    store.at[pl.ds(base, CHUNK), level],
                    sems.at[chunk, level],
                )
            )
        return out

    def body(slot_ref, dst_ref, count_ref, me_ref, recv_hbm, vals, _, *rest):
        pieces, (recv, store, acc, sems, recv_sem) = rest[:groups], rest[groups:]
        arrive = pltpu.make_async_copy(recv_hbm, recv, recv_sem)
        arrive.start()
        for chunk in range(chunks):
            for copy in copies(vals, store, sems, chunk):
                copy.start()
        acc[...] = jnp.zeros_like(acc)
        count = count_ref[0]
        arrive.wait()
        for chunk in range(chunks):
            waits = copies(vals, store, sems, chunk)
            for copy in waits:
                copy.wait()
            live_levels = len(waits)

            def step(turn, _):
                for k in range(UNROLL):
                    j = chunk * CHUNK + turn * UNROLL + k
                    source = recv[slot_ref[j]]
                    left = store[j, :live_levels].reshape(live_levels * side, side)
                    product = jnp.dot(left, source, preferred_element_type=jnp.float32)
                    for level in range(live_levels):
                        i = j + level * slots
                        place = jnp.where(i < count, dst_ref[i], row_tiles)
                        acc[place] += product[level * side : (level + 1) * side]
                return 0

            lax.fori_loop(0, CHUNK // UNROLL, step, 0)
        for k in range(groups):
            there = (me_ref[0] ^ k) * per
            for tile in range(per):
                pieces[k][tile] = acc[there + tile].astype(pieces[k].dtype)

    return pl.pallas_call(
        body,
        grid_spec=pltpu.PrefetchScalarGridSpec(
            num_scalar_prefetch=4,
            grid=(1,),
            in_specs=[
                pl.BlockSpec(memory_space=pl.ANY),
                pl.BlockSpec(memory_space=pl.ANY),
                pl.BlockSpec(memory_space=pltpu.VMEM),
            ],
            out_specs=[pl.BlockSpec((per, side, cols), lambda i, *_: (0, 0, 0))] * groups,
            scratch_shapes=[
                pltpu.VMEM((slots, side, cols), received.dtype),
                pltpu.VMEM((slots, levels, side, side), tile_vals.dtype),
                pltpu.VMEM((row_tiles + 1, side, cols), jnp.float32),
                pltpu.SemaphoreType.DMA((chunks, levels)),
                pltpu.SemaphoreType.DMA,
            ],
        ),
        out_shape=[jax.ShapeDtypeStruct((per, side, cols), received.dtype)] * groups,
        compiler_params=pltpu.CompilerParams(vmem_limit_bytes=52 << 20),
        cost_estimate=pl.CostEstimate(
            flops=8 * entries * side * side * cols,
            bytes_accessed=entries * side * side * 2 + (slots + row_tiles) * side * cols * 2,
            transcendentals=0,
        ),
        name="aggregate",
    )(src_slot, dst_tile, tile_count, me, received, tile_vals, after)


def finish(agg, inputs, me, g_target, w_fwd, b_fwd, w_inv1, b_inv1, w_inv2, b_inv2):
    groups = len(agg)
    rows, cols = agg[0].shape
    width = groups * cols
    block = 256

    def body(me_ref, *refs):
        agg_refs, in_refs = refs[:groups], refs[groups : 2 * groups]
        gt_ref, wf, bf, w1, b1, w2, b2, hid_ref, out_ref, rows_agg, rows_in = refs[2 * groups :]
        for k in range(groups):
            where = pl.ds(pl.multiple_of((me_ref[0] ^ k) * cols, cols), cols)
            rows_agg[:, where] = agg_refs[k][...]
            rows_in[:, where] = in_refs[k][...]
        hidden = jnp.tanh(
            jnp.dot(rows_agg[...], wf[...], preferred_element_type=jnp.float32) + bf[...]
        )
        hidden = hidden.astype(hid_ref.dtype)
        hid_ref[...] = hidden
        inner = jnp.tanh(jnp.dot(hidden, w1[...], preferred_element_type=jnp.float32) + b1[...])
        inner = inner.astype(hid_ref.dtype)
        back = jnp.tanh(jnp.dot(inner, w2[...], preferred_element_type=jnp.float32) + b2[...])
        out_ref[...] = (rows_in[...].astype(jnp.float32) + gt_ref[...] - back).astype(out_ref.dtype)

    piece = pl.BlockSpec((block, cols), lambda i, *_: (i, 0))
    whole = pl.BlockSpec((block, width), lambda i, *_: (i, 0))
    weight = pl.BlockSpec((width, width), lambda i, *_: (0, 0))
    bias = pl.BlockSpec((1, width), lambda i, *_: (0, 0))
    return pl.pallas_call(
        body,
        grid_spec=pltpu.PrefetchScalarGridSpec(
            num_scalar_prefetch=1,
            grid=(rows // block,),
            in_specs=[piece] * (2 * groups) + [whole, weight, bias, weight, bias, weight, bias],
            out_specs=[whole, whole],
            scratch_shapes=[pltpu.VMEM((block, width), agg[0].dtype)] * 2,
        ),
        out_shape=[jax.ShapeDtypeStruct((rows, width), agg[0].dtype)] * 2,
        compiler_params=pltpu.CompilerParams(vmem_limit_bytes=40 << 20),
        cost_estimate=pl.CostEstimate(
            flops=6 * rows * width * width,
            bytes_accessed=6 * width * width + 12 * rows * width,
            transcendentals=3 * rows * width,
        ),
        name="finish",
    )(me, *agg, *inputs, g_target, w_fwd, b_fwd[None], w_inv1, b_inv1[None], w_inv2, b_inv2[None])


def exchange(pieces, groups):
    order = [k for k in range(groups) if k % 2] + [k for k in range(2, groups, 2)]
    back = [pieces[0]] + [None] * (groups - 1)
    for k in order:
        back[k] = lax.ppermute(pieces[k], "section", [(s, s ^ k) for s in range(groups)])
    return back


def swap(piece, k, groups):
    return lax.ppermute(piece, "section", [(s, s ^ k) for s in range(groups)])


def per_device(
    feats,
    tile_vals,
    src_slot,
    dst_tile,
    tile_count,
    send_tile,
    w_fwd,
    b_fwd,
    w_inv1,
    b_inv1,
    w_inv2,
    b_inv2,
    target,
):
    node_rows, feat_cols = feats.shape
    side = tile_vals.shape[1]
    row_tiles = node_rows // side
    rows = target.shape[0]
    groups = node_rows // rows
    me = lax.axis_index("section").astype(jnp.int32)[None]
    tiles = feats.reshape(row_tiles, side, feat_cols)
    outgoing = pack_tiles(tiles, send_tile[0])
    received = lax.all_to_all(outgoing, "dom", split_axis=0, concat_axis=0, tiled=True)
    inner = jnp.tanh(jnp.dot(target, w_inv1, preferred_element_type=jnp.float32) + b_inv1).astype(
        jnp.bfloat16
    )
    g_target = jnp.tanh(jnp.dot(inner, w_inv2, preferred_element_type=jnp.float32) + b_inv2)
    far, near = own_pieces(tiles, me, groups)
    near = [near[0]] + [swap(near[m], 2 * m, groups) for m in range(1, groups // 2)]
    far, after = lax.optimization_barrier((far, received[0, :8] + g_target[:8, :feat_cols]))
    far = swap(far, 1, groups)
    agg = aggregate(
        received, tile_vals, after, src_slot, dst_tile, tile_count, me, row_tiles, groups
    )
    input_rows = [near[0], far[0]]
    for m in range(1, groups // 2):
        input_rows += [near[m], swap(far[m], 2 * m, groups)]
    agg_rows = exchange(agg, groups)
    flat = lambda pieces: [p.reshape(rows, feat_cols) for p in pieces]
    hidden, shifted = finish(
        flat(agg_rows), flat(input_rows), me, g_target, w_fwd, b_fwd, w_inv1, b_inv1, w_inv2, b_inv2
    )
    return (hidden, shifted)


def solution(mesh):
    placed = (
        P("dom", "section"),
        P("dom", None, None),
        P("dom"),
        P("dom"),
        P("dom"),
        P("dom", None),
        P(),
        P(),
        P(),
        P(),
        P(),
        P(),
        P(("dom", "section"), None),
    )
    return jax.shard_map(
        per_device,
        mesh=mesh,
        in_specs=placed,
        out_specs=(P(("dom", "section"), None), P(("dom", "section"), None)),
        check_vma=False,
    )
```
